32 devices in a mesh: row: 8 (over y, x, core), rep: 4 (over z).
Axes of the slice: x: 2, y: 2, z: 4, core: 2. Of those that a mesh axis runs over, the one named last changes fastest.
Arguments:
- features: bfloat16 [8192, 256], P('row'), may hold values from -6 to 6
- weight_self: bfloat16 [256, 256], replicated, may hold values from -0.375 to 0.375
- weight_neigh: bfloat16 [256, 256], replicated, may hold values from -0.375 to 0.375
- degrees: int32 [8192], P('row'), may hold values from 1 to 47
- tile_values: bfloat16 [8, 8, 48, 128, 128], P('row', 'rep'), may hold values from 0 to 1
- tile_blocks: int32 [8, 8, 48, 2], P('row', 'rep'), may hold values from 0 to 7
- tile_count: int32 [8, 8], P('row', 'rep'), may hold values from 1 to 48, as said below
- cotangent: bfloat16 [8192, 256], P(('row', 'rep')), may hold values from -6 to 6
Outputs:
- output: bfloat16 [8192, 256], P(('row', 'rep'))
- grad_self: float32 [256, 256], replicated
- grad_neigh: float32 [256, 256], replicated
- grad_features: bfloat16 [8192, 256], P(('row', 'rep'))
The draws below stay inside these ranges and needn't reach their ends.
Inputs may be any that keep to these rules, and one draw needn't show every extreme that they name: `tile_count`: for some row index and section all 48 slots are live in every draw.
All inputs are finite; a program needn't handle non-finite values.
Results may differ from the reference program's by a relative error of at most 0.024.
Values may be sent and summed in bfloat16 or wider, within the bound.
A program may use at most 64 MiB of HBM per device.

```python
import jax
import jax.numpy as jnp
from jax import lax

FEAT = 256
HID = 256
TILE = 128
BLK_DEV = 8
TCAP = 48
NODES_DEV = 1024
NODES = 8192
SECTIONS = 8


def draw_tile_count(key, part):
    base = jax.random.randint(jax.random.fold_in(key, 11), (SECTIONS, SECTIONS), 1, TCAP // 4 + 1)
    section_load = jax.random.randint(jax.random.fold_in(key, 12), (1, SECTIONS), 1, 5)
    count = jnp.minimum(base * section_load, TCAP)
    return count.at[0, 0].set(TCAP).astype(jnp.int32)


def touch_ends(result, key, low, largest):
    index_at = [jax.random.randint(jax.random.fold_in(key, axis), (), 0, length) for axis, length in enumerate(result.shape)]
    widest = result.shape.index(max(result.shape))
    next_to = index_at[:widest] + [(index_at[widest] + 1) % result.shape[widest]] + index_at[widest + 1:]
    return result.at[tuple(index_at)].set(low).at[tuple(next_to)].set(largest)


def block_levels(stream_key, dims, pieces, smallest, high):
    factor_of = 1.0
    for axis_at, shards_of in pieces:
        draws = jax.random.uniform(jax.random.fold_in(jax.random.fold_in(stream_key, 6), axis_at), (shards_of,), jnp.float32, smallest / len(pieces), high / len(pieces))
        factor_of = factor_of * jnp.repeat(jnp.exp(draws), dims[axis_at] // shards_of).reshape((-1,) + (1,) * (len(dims) - 1 - axis_at))
    return factor_of


def scatter_about(key, shape, width, most, cuts=(), dtype=jnp.bfloat16):
    drawn = jax.random.normal(key, shape, jnp.float32) * width
    if len(cuts) > 0:
        drawn = block_levels(key, shape, cuts, -0.22, 0.18) * drawn
    return jnp.clip(drawn, min=-most, max=most).astype(dtype)


def setup_inputs(seed: int = 0) -> dict:
    seeds = jax.random.split(jax.random.key(seed), 9)
    return {
        "features": scatter_about(seeds[0], (NODES, FEAT), 1.0, 6.0, ((0, 8),)),
        "weight_self": scatter_about(seeds[1], (FEAT, HID), FEAT ** -0.5, 0.375),
        "weight_neigh": scatter_about(seeds[2], (FEAT, HID), FEAT ** -0.5, 0.375),
        "degrees": touch_ends(jax.random.randint(seeds[3], (NODES,), 1, 48), jax.random.fold_in(seeds[3], 1), 1, 47).astype(jnp.int32),
        "tile_values": jnp.clip(1.0 * jax.random.uniform(seeds[4], (SECTIONS, SECTIONS, TCAP, TILE, TILE), jnp.float32) ** block_levels(seeds[4], (SECTIONS, SECTIONS, TCAP, TILE, TILE), ((0, 8), (1, 4)), -0.2, 0.2), 0.0, 1.0).astype(jnp.bfloat16),
        "tile_blocks": touch_ends(jax.random.randint(seeds[5], (SECTIONS, SECTIONS, TCAP, 2), 0, BLK_DEV), jax.random.fold_in(seeds[5], 1), 0, BLK_DEV - 1).astype(jnp.int32),
        "tile_count": draw_tile_count(jax.random.fold_in(seeds[8], 71), 0),
        "cotangent": scatter_about(seeds[7], (NODES, HID), 1.0, 6.0, ((0, 32),)),
    }


def hot_tables(blocks, count):
    live = (jnp.arange(TCAP)[None, :] < count[:, None]).astype(jnp.float32)
    dest_hot = (blocks[..., 0][..., None] == jnp.arange(BLK_DEV)[None, None, :]).astype(jnp.float32) * live[..., None]
    src_hot = (blocks[..., 1][..., None] == jnp.arange(BLK_DEV)[None, None, :]).astype(jnp.float32)
    return dest_hot, src_hot


def reference(features, weight_self, weight_neigh, degrees, tile_values, tile_blocks, tile_count, cotangent):
    feat_blocks = features.astype(jnp.float32).reshape(SECTIONS, BLK_DEV, TILE, FEAT)

    def forward_row(index):
        vals = tile_values[index].astype(jnp.float32)
        dest_hot, src_hot = hot_tables(tile_blocks[index], tile_count[index])
        picked = jnp.einsum('stc,scif->stif', src_hot, feat_blocks)
        prod = jnp.einsum('stij,stjf->stif', vals, picked)
        return jnp.einsum('stb,stif->bif', dest_hot, prod).reshape(NODES_DEV, FEAT)

    agg_sum = lax.map(forward_row, jnp.arange(SECTIONS)).reshape(NODES, FEAT)
    degree = degrees.astype(jnp.float32)[:, None]
    agg = (agg_sum / degree).astype(jnp.bfloat16)
    pre = jnp.dot(features, weight_self, preferred_element_type=jnp.float32) + jnp.dot(agg, weight_neigh, preferred_element_type=jnp.float32)
    output = jax.nn.silu(pre).astype(jnp.bfloat16)
    sig = jax.nn.sigmoid(pre)
    gpre = (cotangent.astype(jnp.float32) * sig * (1.0 + pre * (1.0 - sig))).astype(jnp.bfloat16)
    grad_self = jnp.dot(features.T, gpre, preferred_element_type=jnp.float32)
    grad_neigh = jnp.dot(agg.T, gpre, preferred_element_type=jnp.float32)
    dagg = (jnp.dot(gpre, weight_neigh.T, preferred_element_type=jnp.float32) / degree).astype(jnp.bfloat16)
    dagg_blocks = dagg.astype(jnp.float32).reshape(SECTIONS, BLK_DEV, TILE, FEAT)

    def back_row(total, index):
        vals = tile_values[index].astype(jnp.float32)
        dest_hot, src_hot = hot_tables(tile_blocks[index], tile_count[index])
        picked = jnp.einsum('stb,bif->stif', dest_hot, dagg_blocks[index])
        contrib = jnp.einsum('stij,stif->stjf', vals, picked)
        return total + jnp.einsum('stc,stjf->scjf', src_hot, contrib), None

    start = jnp.zeros((SECTIONS, BLK_DEV, TILE, FEAT), jnp.float32)
    back_total, unused = lax.scan(back_row, start, jnp.arange(SECTIONS))
    back_sum = back_total.reshape(NODES, FEAT).astype(jnp.bfloat16)
    grad_features = (jnp.dot(gpre, weight_self.T, preferred_element_type=jnp.float32) + back_sum.astype(jnp.float32)).astype(jnp.bfloat16)
    return (output, grad_self, grad_neigh, grad_features)
```

```python
import functools

import jax
import jax.numpy as jnp
from jax import lax
from jax.experimental import pallas as pl
from jax.experimental.pallas import tpu as pltpu
from jax.sharding import PartitionSpec as P

MESH = pl.DeviceIdType.MESH
F32 = jnp.float32
BF16 = jnp.bfloat16
PAIR = 2


def dense_kernel(blocks_ref, count_ref, tiles_ref, out_ref, acc):
    section = pl.program_id(0)
    tile = tiles_ref.shape[-1]
    acc[...] = jnp.zeros_like(acc)

    def add(slot, carry):
        to = pl.multiple_of(blocks_ref[section, slot, 0] * tile, tile)
        src = pl.multiple_of(blocks_ref[section, slot, 1] * tile, tile)
        acc[pl.ds(to, tile), pl.ds(src, tile)] += tiles_ref[0, slot].astype(F32)
        return carry

    lax.fori_loop(0, count_ref[section], add, 0)
    out_ref[0] = acc[...].astype(BF16)


def dense_adjacency(tile_values, tile_blocks, tile_count, rows):
    sections, slots, tile, _ = tile_values.shape
    return pl.pallas_call(
        dense_kernel,
        grid=(sections,),
        out_shape=jax.ShapeDtypeStruct((sections, rows, rows), BF16),
        in_specs=[
            pl.BlockSpec(memory_space=pltpu.SMEM),
            pl.BlockSpec(memory_space=pltpu.SMEM),
            pl.BlockSpec((1, slots, tile, tile), lambda s: (s, 0, 0, 0)),
        ],
        out_specs=pl.BlockSpec((1, rows, rows), lambda s: (s, 0, 0)),
        scratch_shapes=[pltpu.VMEM((rows, rows), F32)],
        name="dense",
    )(tile_blocks, tile_count, tile_values)


def remote(src, dst, send, recv, device):
    return pltpu.make_async_remote_copy(
        src_ref=src, dst_ref=dst, send_sem=send, recv_sem=recv, device_id=device, device_id_type=MESH
    )


def layer_kernel(
    nrow, nrep, here,
    feat, wself, wneigh, deg, cot, adj_hbm,
    out, gself, gneigh, gfeat,
    adj, src, part, part_in, dagg, dagg_t, terms, pair_in, summed, plane_in, back, back_in,
    wpart, wrow_in, wrep_in, wall, base,
    adj_sem, loc_sem, a1s, a1r, a2s, a2r, a3s, a3r, bs, br, cs, cr, w1s, w1r, w2s, w2r, w3s, w3r,
    d0s, d0r, d1s, d1r, d2s, d2r,
):
    row, rep = lax.axis_index("row"), lax.axis_index("rep")
    rows, width = feat.shape
    share = rows // nrep
    half = nrow // PAIR
    hi, lo = row // PAIR, row % PAIR
    partner = (hi * PAIR + (1 - lo), rep)
    owner = (rep * here + row // nrep, row % nrep)
    giver = ((row % here) * nrep + rep, row // here)
    moves = jnp.logical_or(owner[0] != row, owner[1] != rep)

    adj_copy = pltpu.make_async_copy(adj_hbm, adj, adj_sem)
    adj_copy.start()

    barrier = pltpu.get_barrier_semaphore()

    def greet(device):
        pl.semaphore_signal(barrier, inc=1, device_id=device, device_id_type=MESH)

    for d in range(1, nrow):
        greet(((row + d) % nrow, rep))
    for d in range(1, nrep):
        greet((row, (rep + d) % nrep))

    @pl.when(moves)
    def _():
        greet(owner)
        greet(giver)

    pl.semaphore_wait(barrier, nrow - 1 + nrep - 1 + 2 * moves.astype(jnp.int32))

    is_source = row // here == rep
    first = (row - rep * here) * nrep
    own_chunk = row == rep * here + row // nrep

    def scatter(q):
        return remote(
            feat.at[pl.ds(q * share, share)], src.at[first + q], a1s.at[q], a1r.at[0], (first + q, rep)
        )

    for q in range(nrep):
        @pl.when(jnp.logical_and(is_source, first + q != row))
        def _():
            scatter(q).start()

        @pl.when(jnp.logical_and(is_source, first + q == row))
        def _():
            local = pltpu.make_async_copy(feat.at[pl.ds(q * share, share)], src.at[row], loc_sem)
            local.start()
            local.wait()

    my_feat = feat[pl.ds(pl.multiple_of(rep * share, share), share), :]
    base[...] = jnp.dot(my_feat, wself[...], preferred_element_type=F32)

    @pl.when(jnp.logical_not(own_chunk))
    def _():
        remote(src.at[row], src.at[row], a1s.at[0], a1r.at[0], partner).wait_recv()

    def gather(d):
        to = ((hi + d) % half) * PAIR + lo
        return remote(src.at[row], src.at[row], a2s.at[d - 1], a2r.at[d - 1], (to, rep))

    def share_pair(d):
        chunk = ((hi + half - d) % half) * PAIR + lo
        return remote(src.at[chunk], src.at[chunk], a3s.at[d], a3r.at[d], partner)

    for d in range(1, half):
        gather(d).start()
    share_pair(0).start()
    for d in range(1, half):
        gather(d).wait_recv()
        share_pair(d).start()
    for d in range(half):
        share_pair(d).wait_recv()
    adj_copy.wait()

    def partial(q):
        total = jnp.zeros((share, width), F32)
        for j in range(here):
            a = adj[j, pl.ds(pl.multiple_of(q * share, share), share), :]
            f = src[pl.ds(j * nrep, nrep)].reshape(rows, width)
            total = total + jnp.dot(a, f, preferred_element_type=F32)
        return total

    def send_part(d):
        to = (rep + d) % nrep
        return remote(part.at[d - 1], part_in.at[d - 1], bs.at[d - 1], br.at[d - 1], (row, to))

    for d in range(1, nrep):
        part[d - 1] = partial((rep + d) % nrep).astype(BF16)
        send_part(d).start()
    total = partial(rep)
    for d in range(1, nrep):
        send_part(d).wait_recv()
        total = total + part_in[d - 1].astype(F32)

    degree = deg[...]
    agg = (total / degree).astype(BF16)
    pre = base[...] + jnp.dot(agg, wneigh[...], preferred_element_type=F32)
    sig = jax.nn.sigmoid(pre)
    gpre = (cot[...].astype(F32) * sig * (1.0 + pre * (1.0 - sig))).astype(BF16)
    back_t = lax.dot_general(gpre, wneigh[...], (((1,), (1,)), ((), ())), preferred_element_type=F32)
    dagg[rep] = (back_t / degree).astype(BF16)

    def send_dagg(d):
        return remote(
            dagg.at[rep], dagg.at[rep], cs.at[d - 1], cr.at[d - 1], (row, (rep + d) % nrep)
        )

    for d in range(1, nrep):
        send_dagg(d).start()
    out[...] = (pre * sig).astype(BF16)
    ws = lax.dot_general(my_feat, gpre, (((0,), (0,)), ((), ())), preferred_element_type=F32)
    wn = lax.dot_general(agg, gpre, (((0,), (0,)), ((), ())), preferred_element_type=F32)
    piece = wpart.shape[1]
    wpart[pl.ds(0, half)] = ws.astype(BF16).reshape(half, piece, width)
    wpart[pl.ds(half, half)] = wn.astype(BF16).reshape(half, piece, width)

    def send_w1(d):
        to = (row + d) % nrow
        return remote(wpart.at[to], wrow_in.at[d - 1], w1s.at[d - 1], w1r.at[d - 1], (to, rep))

    for d in range(1, nrow):
        send_w1(d).start()
    base[...] = lax.dot_general(gpre, wself[...], (((1,), (1,)), ((), ())), preferred_element_type=F32)
    for d in range(1, nrep):
        remote(
            dagg.at[rep], dagg.at[(rep + nrep - d) % nrep], cs.at[d - 1], cr.at[d - 1], (row, rep)
        ).wait_recv()
    dagg_t[...] = dagg[...].reshape(rows, width).T

    unit = max(share, 128)
    per_unit = unit // share

    def send_pair(h):
        return remote(
            terms.at[h * PAIR + (1 - lo)], pair_in.at[h], d0s.at[h], d0r.at[h], partner
        )

    for u in range(here * rows // unit):
        j, col = divmod(u * unit, rows)
        t = jnp.dot(dagg_t[...], adj[j, :, col : col + unit], preferred_element_type=F32)
        terms[pl.ds(u * per_unit, per_unit)] = t.T.astype(BF16).reshape(per_unit, share, width)
        for r in range(u * per_unit, (u + 1) * per_unit):
            @pl.when(r % PAIR != lo)
            def _():
                send_pair(r // PAIR).start()

    wsum = wpart[row].astype(F32)
    for d in range(1, nrow):
        send_w1(d).wait_recv()
        wsum = wsum + wrow_in[d - 1].astype(F32)
    wrep_in[rep] = wsum.astype(BF16)

    def send_w2(d):
        return remote(
            wrep_in.at[rep], wrep_in.at[rep], w2s.at[d - 1], w2r.at[d - 1], (row, (rep + d) % nrep)
        )

    for d in range(1, nrep):
        send_w2(d).start()

    def send_plane(d):
        h = (hi + d) % half
        return remote(
            summed.at[h], plane_in.at[d - 1], d1s.at[d - 1], d1r.at[d - 1], (h * PAIR + lo, rep)
        )

    for d in list(range(1, half)) + [0]:
        h = (hi + d) % half
        send_pair(h).wait_recv()
        both = terms[h * PAIR + lo].astype(F32) + pair_in[h].astype(F32)
        if d > 0:
            summed[h] = both.astype(BF16)
            send_plane(d).start()

    for d in range(1, nrep):
        remote(
            wrep_in.at[rep], wrep_in.at[(rep + nrep - d) % nrep], w2s.at[d - 1], w2r.at[d - 1], (row, rep)
        ).wait_recv()
    wsum = wrep_in[0].astype(F32)
    for k in range(1, nrep):
        wsum = wsum + wrep_in[k].astype(F32)
    wall[row] = wsum.astype(BF16)

    def send_w3(d):
        return remote(
            wall.at[row], wall.at[row], w3s.at[d - 1], w3r.at[d - 1], ((row + d) % nrow, rep)
        )

    for d in range(1, nrow):
        send_w3(d).start()

    for d in range(1, half):
        send_plane(d).wait_recv()
        both = both + plane_in[d - 1].astype(F32)
    back[...] = both.astype(BF16)
    to_owner = remote(back, back_in, d2s, d2r, owner)

    @pl.when(moves)
    def _():
        to_owner.start()

    for d in range(1, nrow):
        remote(
            wall.at[row], wall.at[(row + nrow - d) % nrow], w3s.at[d - 1], w3r.at[d - 1], (row, rep)
        ).wait_recv()
    gself[...] = wall[pl.ds(0, half)].reshape(width, width).astype(F32)
    gneigh[...] = wall[pl.ds(half, half)].reshape(width, width).astype(F32)

    @pl.when(moves)
    def _():
        to_owner.wait_recv()
        gfeat[...] = (base[...] + back_in[...].astype(F32)).astype(BF16)

    @pl.when(jnp.logical_not(moves))
    def _():
        gfeat[...] = (base[...] + back[...].astype(F32)).astype(BF16)

    for q in range(nrep):
        @pl.when(jnp.logical_and(is_source, first + q != row))
        def _():
            scatter(q).wait_send()

    for d in range(1, half):
        gather(d).wait_send()
        send_plane(d).wait_send()
    for d in range(half):
        share_pair(d).wait_send()
        send_pair(d).wait_send()
    for d in range(1, nrep):
        send_part(d).wait_send()
        send_dagg(d).wait_send()
        send_w2(d).wait_send()
    for d in range(1, nrow):
        send_w1(d).wait_send()
        send_w3(d).wait_send()

    @pl.when(moves)
    def _():
        to_owner.wait_send()


def body(
    nrow, nrep,
    features, weight_self, weight_neigh, degrees, tile_values, tile_blocks, tile_count, cotangent,
):
    rows, width = features.shape
    here = tile_values.shape[1]
    share = rows // nrep
    half = nrow // PAIR
    piece = 2 * width // nrow
    adjacency = dense_adjacency(tile_values[0], tile_blocks[0], tile_count[0], rows)
    degree = lax.dynamic_slice_in_dim(degrees, lax.axis_index("rep") * share, share, 0)
    degree = degree.astype(F32)[:, None]
    sems = pltpu.SemaphoreType.DMA
    vmem = pl.BlockSpec(memory_space=pltpu.VMEM)
    return pl.pallas_call(
        functools.partial(layer_kernel, nrow, nrep, here),
        out_shape=(
            jax.ShapeDtypeStruct((share, width), BF16),
            jax.ShapeDtypeStruct((width, width), F32),
            jax.ShapeDtypeStruct((width, width), F32),
            jax.ShapeDtypeStruct((share, width), BF16),
        ),
        in_specs=[vmem] * 5 + [pl.BlockSpec(memory_space=pl.ANY)],
        out_specs=(vmem,) * 4,
        scratch_shapes=[
            pltpu.VMEM((here, rows, rows), BF16),
            pltpu.VMEM((nrow, share, width), BF16),
            pltpu.VMEM((nrep - 1, share, width), BF16),
            pltpu.VMEM((nrep - 1, share, width), BF16),
            pltpu.VMEM((nrep, share, width), BF16),
            pltpu.VMEM((width, rows), BF16),
            pltpu.VMEM((nrow, share, width), BF16),
            pltpu.VMEM((half, share, width), BF16),
            pltpu.VMEM((half, share, width), BF16),
            pltpu.VMEM((half - 1, share, width), BF16),
            pltpu.VMEM((share, width), BF16),
            pltpu.VMEM((share, width), BF16),
            pltpu.VMEM((nrow, piece, width), BF16),
            pltpu.VMEM((nrow - 1, piece, width), BF16),
            pltpu.VMEM((nrep, piece, width), BF16),
            pltpu.VMEM((nrow, piece, width), BF16),
            pltpu.VMEM((share, width), F32),
            sems, sems,
            sems((nrep,)), sems((1,)),
            sems((half - 1,)), sems((half - 1,)),
            sems((half,)), sems((half,)),
            sems((nrep - 1,)), sems((nrep - 1,)),
            sems((nrep - 1,)), sems((nrep - 1,)),
            sems((nrow - 1,)), sems((nrow - 1,)),
            sems((nrep - 1,)), sems((nrep - 1,)),
            sems((nrow - 1,)), sems((nrow - 1,)),
            sems((half,)), sems((half,)),
            sems((half - 1,)), sems((half - 1,)),
            sems, sems,
        ],
        compiler_params=pltpu.CompilerParams(collective_id=0, has_side_effects=True),
        name="layer",
    )(features, weight_self, weight_neigh, degree, cotangent, adjacency)


def solution(mesh):
    in_specs = (
        P("row", None),
        P(),
        P(),
        P("row"),
        P("row", "rep", None, None, None),
        P("row", "rep", None, None),
        P("row", "rep"),
        P(("row", "rep"), None),
    )
    out_specs = (P(("row", "rep"), None), P(), P(), P(("row", "rep"), None))
    run = functools.partial(body, mesh.shape["row"], mesh.shape["rep"])
    return jax.shard_map(run, mesh=mesh, in_specs=in_specs, out_specs=out_specs, check_vma=False)
```

```python
import functools

import jax
import jax.numpy as jnp
from jax import lax
from jax.experimental import pallas as pl
from jax.experimental.pallas import tpu as pltpu
from jax.sharding import PartitionSpec as P

MESH = pl.DeviceIdType.MESH
F32 = jnp.float32
BF16 = jnp.bfloat16
PAIR = 2


def dense_kernel(blocks_ref, count_ref, tiles_ref, out_ref, acc):
    section = pl.program_id(0)
    tile = tiles_ref.shape[-1]
    acc[...] = jnp.zeros_like(acc)

    def add(slot, carry):
        to = pl.multiple_of(blocks_ref[section, 0, slot] * tile, tile)
        src = pl.multiple_of(blocks_ref[section, 1, slot] * tile, tile)
        acc[pl.ds(to, tile), pl.ds(src, tile)] += tiles_ref[0, slot].astype(F32)
        return carry

    lax.fori_loop(0, count_ref[section], add, 0)
    out_ref[0] = acc[...].astype(BF16)


def dense_adjacency(tile_values, tile_blocks, tile_count, rows):
    sections, slots, tile, _ = tile_values.shape
    return pl.pallas_call(
        dense_kernel,
        grid=(sections,),
        out_shape=jax.ShapeDtypeStruct((sections, rows, rows), BF16),
        in_specs=[
            pl.BlockSpec(memory_space=pltpu.SMEM),
            pl.BlockSpec(memory_space=pltpu.SMEM),
            pl.BlockSpec((1, slots, tile, tile), lambda s: (s, 0, 0, 0)),
        ],
        out_specs=pl.BlockSpec((1, rows, rows), lambda s: (s, 0, 0)),
        scratch_shapes=[pltpu.VMEM((rows, rows), F32)],
        name="dense",
    )(tile_blocks, tile_count, tile_values)


def remote(src, dst, send, recv, device):
    return pltpu.make_async_remote_copy(
        src_ref=src, dst_ref=dst, send_sem=send, recv_sem=recv, device_id=device, device_id_type=MESH
    )


def layer_kernel(
    nrow, nrep, here,
    feat, wself, wneigh, deg, cot, adj_hbm,
    out, wall, gfeat,
    adj, own_feat, src, part, part_in, dagg, dagg_t, terms, pair_in, summed, plane_in, back, back_in,
    wpart, wrow_in, wrep_in, base, deg_col,
    adj_sem, loc_sem, a1s, a1r, a2s, a2r, a3s, a3r, bs, br, cs, cr, w1s, w1r, w2s, w2r, w3s, w3r,
    d0s, d0r, d1s, d1r, d2s, d2r,
):
    row, rep = lax.axis_index("row"), lax.axis_index("rep")
    rows, width = feat.shape
    lanes = src.shape[-1]
    slices = width // lanes
    share = rows // nrep
    half = nrow // PAIR
    hi, lo = row // PAIR, row % PAIR
    partner = (hi * PAIR + (1 - lo), rep)
    owner = (rep * here + row // nrep, row % nrep)
    giver = ((row % here) * nrep + rep, row // here)
    moves = jnp.logical_or(owner[0] != row, owner[1] != rep)

    adj_copy = pltpu.make_async_copy(adj_hbm, adj, adj_sem)
    adj_copy.start()

    barrier = pltpu.get_barrier_semaphore()

    def greet(device):
        pl.semaphore_signal(barrier, inc=1, device_id=device, device_id_type=MESH)

    for d in range(1, nrow):
        greet(((row + d) % nrow, rep))
    for d in range(1, nrep):
        greet((row, (rep + d) % nrep))

    @pl.when(moves)
    def _():
        greet(owner)
        greet(giver)

    for c in range(slices):
        own_feat[c] = feat[:, c * lanes : (c + 1) * lanes]

    pl.semaphore_wait(barrier, nrow - 1 + nrep - 1 + 2 * moves.astype(jnp.int32))

    is_source = row // here == rep
    first = (row - rep * here) * nrep
    own_chunk = row == rep * here + row // nrep

    def scatter(c, q):
        return remote(
            own_feat.at[c, pl.ds(q * share, share)], src.at[c, first + q],
            a1s.at[c, q], a1r.at[c], (first + q, rep),
        )

    for c in range(slices):
        for q in range(nrep):
            @pl.when(jnp.logical_and(is_source, first + q != row))
            def _():
                scatter(c, q).start()

            @pl.when(jnp.logical_and(is_source, first + q == row))
            def _():
                local = pltpu.make_async_copy(
                    own_feat.at[c, pl.ds(q * share, share)], src.at[c, row], loc_sem
                )
                local.start()
                local.wait()

    def gather(c, d):
        to = ((hi + d) % half) * PAIR + lo
        return remote(
            src.at[c, row], src.at[c, row], a2s.at[c, d - 1], a2r.at[c, d - 1], (to, rep)
        )

    def share_pair(c, d):
        chunk = ((hi + half - d) % half) * PAIR + lo
        return remote(src.at[c, chunk], src.at[c, chunk], a3s.at[c, d], a3r.at[c, d], partner)

    for c in range(slices):
        @pl.when(jnp.logical_not(own_chunk))
        def _():
            remote(src.at[c, row], src.at[c, row], a1s.at[c, 0], a1r.at[c], partner).wait_recv()

        for d in range(1, half):
            gather(c, d).start()
        share_pair(c, 0).start()

    my_feat = feat[pl.ds(pl.multiple_of(rep * share, share), share), :]
    base[...] = jnp.dot(my_feat, wself[...], preferred_element_type=F32)
    run = deg.shape[1]
    for b in range(rows // run):
        line = jnp.broadcast_to(deg[b : b + 1, :].astype(F32), (run, run))
        deg_col[pl.ds(b * run, run), :] = line.T
    adj_copy.wait()

    def partial(c, q):
        total = jnp.zeros((share, lanes), F32)
        for j in range(here):
            a = adj[j, pl.ds(pl.multiple_of(q * share, share), share), :]
            f = src[c, pl.ds(j * nrep, nrep)].reshape(rows, lanes)
            total = total + jnp.dot(a, f, preferred_element_type=F32)
        return total

    def send_part(c, d):
        to = (rep + d) % nrep
        return remote(
            part.at[c, d - 1], part_in.at[c, d - 1], bs.at[c, d - 1], br.at[c, d - 1], (row, to)
        )

    for c in range(slices):
        for d in range(1, half):
            gather(c, d).wait_recv()
            share_pair(c, d).start()
        for d in range(half):
            share_pair(c, d).wait_recv()
        for d in range(1, nrep):
            part[c, d - 1] = partial(c, (rep + d) % nrep).astype(BF16)
            send_part(c, d).start()
    degree = deg_col[pl.ds(pl.multiple_of(rep * share, share), share), :]
    aggs = []
    for c in range(slices):
        total = partial(c, rep)
        for d in range(1, nrep):
            send_part(c, d).wait_recv()
            total = total + part_in[c, d - 1].astype(F32)
        aggs.append((total / degree).astype(BF16))
    agg = jnp.concatenate(aggs, axis=1)

    pre = base[...] + jnp.dot(agg, wneigh[...], preferred_element_type=F32)
    sig = jax.nn.sigmoid(pre)
    gpre = (cot[...].astype(F32) * sig * (1.0 + pre * (1.0 - sig))).astype(BF16)

    def send_dagg(c, d):
        return remote(
            dagg.at[c, rep], dagg.at[c, rep], cs.at[c, d - 1], cr.at[c, d - 1],
            (row, (rep + d) % nrep),
        )

    for c in range(slices):
        back_t = lax.dot_general(
            gpre, wneigh[c * lanes : (c + 1) * lanes, :], (((1,), (1,)), ((), ())),
            preferred_element_type=F32,
        )
        dagg[c, rep] = (back_t / degree).astype(BF16)
        for d in range(1, nrep):
            send_dagg(c, d).start()
    ws = lax.dot_general(my_feat, gpre, (((0,), (0,)), ((), ())), preferred_element_type=F32)
    wn = lax.dot_general(agg, gpre, (((0,), (0,)), ((), ())), preferred_element_type=F32)
    piece = wpart.shape[1]
    wpart[pl.ds(0, half)] = ws.astype(BF16).reshape(half, piece, width)
    wpart[pl.ds(half, half)] = wn.astype(BF16).reshape(half, piece, width)

    def send_w1(d):
        to = (row + d) % nrow
        return remote(wpart.at[to], wrow_in.at[d - 1], w1s.at[d - 1], w1r.at[d - 1], (to, rep))

    for d in range(1, nrow):
        send_w1(d).start()
    out[...] = (pre * sig).astype(BF16)
    base[...] = lax.dot_general(gpre, wself[...], (((1,), (1,)), ((), ())), preferred_element_type=F32)

    unit = max(share, 128)
    per_unit = unit // share

    def send_pair(c, h):
        return remote(
            terms.at[c, h * PAIR + (1 - lo)], pair_in.at[c, h], d0s.at[c, h], d0r.at[c, h], partner
        )

    def send_plane(c, d):
        h = (hi + d) % half
        return remote(
            summed.at[c, h], plane_in.at[c, d - 1], d1s.at[c, d - 1], d1r.at[c, d - 1],
            (h * PAIR + lo, rep),
        )

    def to_owner(c):
        return remote(back.at[c], back_in.at[c], d2s.at[c], d2r.at[c], owner)

    def make_terms(c):
        for d in range(1, nrep):
            remote(
                dagg.at[c, rep], dagg.at[c, (rep + nrep - d) % nrep], cs.at[c, d - 1], cr.at[c, d - 1],
                (row, rep),
            ).wait_recv()
        dagg_t[...] = dagg[c].reshape(rows, lanes).T
        for u in range(here * rows // unit):
            j, col = divmod(u * unit, rows)
            t = jnp.dot(dagg_t[...], adj[j, :, col : col + unit], preferred_element_type=F32)
            terms[c, pl.ds(u * per_unit, per_unit)] = t.T.astype(BF16).reshape(per_unit, share, lanes)
            for r in range(u * per_unit, (u + 1) * per_unit):
                @pl.when(r % PAIR != lo)
                def _():
                    send_pair(c, r // PAIR).start()

    def add_pair(c):
        for d in list(range(1, half)) + [0]:
            h = (hi + d) % half
            send_pair(c, h).wait_recv()
            both = terms[c, h * PAIR + lo].astype(F32) + pair_in[c, h].astype(F32)
            if d > 0:
                summed[c, h] = both.astype(BF16)
                send_plane(c, d).start()
            else:
                back_sum[c] = both

    def add_plane(c):
        both = back_sum[c]
        for d in range(1, half):
            send_plane(c, d).wait_recv()
            both = both + plane_in[c, d - 1].astype(F32)
        back[c] = both.astype(BF16)

        @pl.when(moves)
        def _():
            to_owner(c).start()

    back_sum = {}
    for c in range(slices):
        make_terms(c)
        if c + 1 < slices:
            add_pair(c)

    wsum = wpart[row].astype(F32)
    for d in range(1, nrow):
        send_w1(d).wait_recv()
        wsum = wsum + wrow_in[d - 1].astype(F32)
    wrep_in[rep] = wsum.astype(BF16)

    def send_w2(d):
        return remote(
            wrep_in.at[rep], wrep_in.at[rep], w2s.at[d - 1], w2r.at[d - 1], (row, (rep + d) % nrep)
        )

    for d in range(1, nrep):
        send_w2(d).start()
    add_pair(slices - 1)
    for c in range(slices - 1):
        add_plane(c)

    for d in range(1, nrep):
        remote(
            wrep_in.at[rep], wrep_in.at[(rep + nrep - d) % nrep], w2s.at[d - 1], w2r.at[d - 1], (row, rep)
        ).wait_recv()
    wsum = wrep_in[0].astype(F32)
    for k in range(1, nrep):
        wsum = wsum + wrep_in[k].astype(F32)
    wall[row] = wsum.astype(BF16)

    def send_w3(d):
        return remote(
            wall.at[row], wall.at[row], w3s.at[d - 1], w3r.at[d - 1], ((row + d) % nrow, rep)
        )

    for d in range(1, nrow):
        send_w3(d).start()
    add_plane(slices - 1)
    for d in range(1, nrow):
        remote(
            wall.at[row], wall.at[(row + nrow - d) % nrow], w3s.at[d - 1], w3r.at[d - 1], (row, rep)
        ).wait_recv()

    for c in range(slices):
        cols = slice(c * lanes, (c + 1) * lanes)

        @pl.when(moves)
        def _():
            to_owner(c).wait_recv()
            gfeat[:, cols] = (base[:, cols] + back_in[c].astype(F32)).astype(BF16)

        @pl.when(jnp.logical_not(moves))
        def _():
            gfeat[:, cols] = (base[:, cols] + back[c].astype(F32)).astype(BF16)

    for c in range(slices):
        for q in range(nrep):
            @pl.when(jnp.logical_and(is_source, first + q != row))
            def _():
                scatter(c, q).wait_send()

        for d in range(1, half):
            gather(c, d).wait_send()
            send_plane(c, d).wait_send()
        for d in range(half):
            share_pair(c, d).wait_send()
            send_pair(c, d).wait_send()
        for d in range(1, nrep):
            send_part(c, d).wait_send()
            send_dagg(c, d).wait_send()

        @pl.when(moves)
        def _():
            to_owner(c).wait_send()

    for d in range(1, nrep):
        send_w2(d).wait_send()
    for d in range(1, nrow):
        send_w1(d).wait_send()
        send_w3(d).wait_send()


def close_kernel(out_in, wall, gfeat_in, out, gself, gneigh, gfeat):
    half = wall.shape[0] // 2
    out[...] = out_in[...]
    gfeat[...] = gfeat_in[...]
    gself[...] = wall[pl.ds(0, half)].reshape(gself.shape).astype(F32)
    gneigh[...] = wall[pl.ds(half, half)].reshape(gneigh.shape).astype(F32)


def body(
    nrow, nrep,
    features, weight_self, weight_neigh, degrees, tile_values, tile_blocks, tile_count, cotangent,
):
    rows, width = features.shape
    here = tile_values.shape[1]
    tile = tile_values.shape[-1]
    share = rows // nrep
    half = nrow // PAIR
    piece = 2 * width // nrow
    lanes = 128
    slices = width // lanes
    adjacency = dense_adjacency(
        tile_values[0], tile_blocks.transpose(0, 1, 3, 2)[0], tile_count[0], rows
    )
    sems = pltpu.SemaphoreType.DMA
    vmem = pl.BlockSpec(memory_space=pltpu.VMEM)

    def buf(*shape):
        return pltpu.VMEM(shape, BF16)

    out, wall, gfeat = pl.pallas_call(
        functools.partial(layer_kernel, nrow, nrep, here),
        out_shape=(
            jax.ShapeDtypeStruct((share, width), BF16),
            jax.ShapeDtypeStruct((nrow, piece, width), BF16),
            jax.ShapeDtypeStruct((share, width), BF16),
        ),
        in_specs=[vmem] * 5 + [pl.BlockSpec(memory_space=pl.ANY)],
        out_specs=(vmem,) * 3,
        scratch_shapes=[
            buf(here, rows, rows),
            buf(slices, rows, lanes),
            buf(slices, nrow, share, lanes),
            buf(slices, nrep - 1, share, lanes),
            buf(slices, nrep - 1, share, lanes),
            buf(slices, nrep, share, lanes),
            buf(lanes, rows),
            buf(slices, nrow, share, lanes),
            buf(slices, half, share, lanes),
            buf(slices, half, share, lanes),
            buf(slices, half - 1, share, lanes),
            buf(slices, share, lanes),
            buf(slices, share, lanes),
            buf(nrow, piece, width),
            buf(nrow - 1, piece, width),
            buf(nrep, piece, width),
            pltpu.VMEM((share, width), F32),
            pltpu.VMEM((rows, tile), F32),
            sems, sems,
            sems((slices, nrep)), sems((slices,)),
            sems((slices, half - 1)), sems((slices, half - 1)),
            sems((slices, half)), sems((slices, half)),
            sems((slices, nrep - 1)), sems((slices, nrep - 1)),
            sems((slices, nrep - 1)), sems((slices, nrep - 1)),
            sems((nrow - 1,)), sems((nrow - 1,)),
            sems((nrep - 1,)), sems((nrep - 1,)),
            sems((nrow - 1,)), sems((nrow - 1,)),
            sems((slices, half)), sems((slices, half)),
            sems((slices, half - 1)), sems((slices, half - 1)),
            sems((slices,)), sems((slices,)),
        ],
        compiler_params=pltpu.CompilerParams(collective_id=0, has_side_effects=True),
        name="layer",
    )(features, weight_self, weight_neigh, degrees.reshape(rows // tile, tile), cotangent, adjacency)
    out, grad_self, grad_neigh, gfeat = pl.pallas_call(
        close_kernel,
        out_shape=(
            jax.ShapeDtypeStruct((share, width), BF16),
            jax.ShapeDtypeStruct((width, width), F32),
            jax.ShapeDtypeStruct((width, width), F32),
            jax.ShapeDtypeStruct((share, width), BF16),
        ),
        in_specs=[vmem] * 3,
        out_specs=(vmem,) * 4,
        name="close",
    )(out, wall, gfeat)
    return out, grad_self, grad_neigh, gfeat


def solution(mesh):
    in_specs = (
        P("row", None),
        P(),
        P(),
        P("row"),
        P("row", "rep", None, None, None),
        P("row", "rep", None, None),
        P("row", "rep"),
        P(("row", "rep"), None),
    )
    out_specs = (P(("row", "rep"), None), P(), P(), P(("row", "rep"), None))
    run = functools.partial(body, mesh.shape["row"], mesh.shape["rep"])
    return jax.shard_map(run, mesh=mesh, in_specs=in_specs, out_specs=out_specs, check_vma=False)
```

```python
import functools

import jax
import jax.numpy as jnp
from jax import lax
from jax.experimental import pallas as pl
from jax.experimental.pallas import tpu as pltpu
from jax.sharding import PartitionSpec as P

MESH = pl.DeviceIdType.MESH
F32 = jnp.float32
BF16 = jnp.bfloat16
PAIR = 2


def dense_kernel(blocks_ref, count_ref, tiles_ref, out_ref, acc):
    section = pl.program_id(0)
    tile = tiles_ref.shape[-1]
    acc[...] = jnp.zeros_like(acc)

    def add(slot, carry):
        to = pl.multiple_of(blocks_ref[section, 0, slot] * tile, tile)
        src = pl.multiple_of(blocks_ref[section, 1, slot] * tile, tile)
        acc[pl.ds(to, tile), pl.ds(src, tile)] += tiles_ref[0, slot].astype(F32)
        return carry

    lax.fori_loop(0, count_ref[section], add, 0)
    out_ref[0] = acc[...].astype(BF16)


def dense_adjacency(tile_values, tile_blocks, tile_count, rows):
    sections, slots, tile, _ = tile_values.shape
    return pl.pallas_call(
        dense_kernel,
        grid=(sections,),
        out_shape=jax.ShapeDtypeStruct((sections, rows, rows), BF16),
        in_specs=[
            pl.BlockSpec(memory_space=pltpu.SMEM),
            pl.BlockSpec(memory_space=pltpu.SMEM),
            pl.BlockSpec((1, slots, tile, tile), lambda s: (s, 0, 0, 0)),
        ],
        out_specs=pl.BlockSpec((1, rows, rows), lambda s: (s, 0, 0)),
        scratch_shapes=[pltpu.VMEM((rows, rows), F32)],
        name="dense",
    )(tile_blocks, tile_count, tile_values)


def remote(src, dst, send, recv, device):
    return pltpu.make_async_remote_copy(
        src_ref=src, dst_ref=dst, send_sem=send, recv_sem=recv, device_id=device, device_id_type=MESH
    )


def layer_kernel(
    nrow, nrep, here,
    feat, wself, wneigh, deg, cot, adj_hbm,
    out, wall, gfeat,
    adj, own_feat, src, part, part_in, dagg, dagg_t, terms, pair_in, summed, plane_in, back, back_in,
    wpart, wrow_in, wrep_in, base, deg_col,
    adj_sem, loc_sem, afs, a1s, a1r, a2s, a2r, a3s, a3r, bs, br, cs, fs, cr, w1s, w1r, w2s, w2r, w3s, w3r,
    d0s, d0r, d1s, d1r, d2s, d2r,
):
    row, rep = lax.axis_index("row"), lax.axis_index("rep")
    rows, width = feat.shape
    lanes = src.shape[-1]
    slices = width // lanes
    share = rows // nrep
    half = nrow // PAIR
    hi, lo = row // PAIR, row % PAIR
    partner = (hi * PAIR + (1 - lo), rep)
    owner = (rep * here + row // nrep, row % nrep)
    giver = ((row % here) * nrep + rep, row // here)
    moves = jnp.logical_or(owner[0] != row, owner[1] != rep)

    adj_copy = pltpu.make_async_copy(adj_hbm, adj, adj_sem)
    adj_copy.start()

    barrier = pltpu.get_barrier_semaphore()

    def greet(device):
        pl.semaphore_signal(barrier, inc=1, device_id=device, device_id_type=MESH)

    for d in range(1, nrow):
        greet(((row + d) % nrow, rep))
    for d in range(1, nrep):
        greet((row, (rep + d) % nrep))

    @pl.when(moves)
    def _():
        greet(owner)
        greet(giver)

    def is_far(r, k):
        return r // PAIR == half - 1 - (k * here) // PAIR

    other = (rep + nrep - nrep // 2) % nrep
    far_first = (row - other * here) * nrep
    serves_far = row // here == other
    far_me = is_far(row, rep)
    far_source = (rep * here + row // nrep, (rep + nrep // 2) % nrep)

    def sends_far(q):
        return jnp.logical_and(serves_far, is_far(far_first + q, other))

    expected = nrow - 1 + nrep - 1 + 2 * moves.astype(jnp.int32) + far_me.astype(jnp.int32)
    for q in range(nrep):
        expected = expected + sends_far(q).astype(jnp.int32)

        @pl.when(sends_far(q))
        def _():
            greet((far_first + q, other))

    @pl.when(far_me)
    def _():
        greet(far_source)

    for c in range(slices):
        own_feat[c] = feat[:, c * lanes : (c + 1) * lanes]

    pl.semaphore_wait(barrier, expected)

    is_source = row // here == rep
    first = (row - rep * here) * nrep
    own_chunk = jnp.logical_and(row == rep * here + row // nrep, jnp.logical_not(far_me))

    def sends_near(q):
        near = jnp.logical_and(is_source, jnp.logical_not(is_far(first + q, rep)))
        return jnp.logical_and(near, first + q != row)

    def scatter_far(c, q):
        return remote(
            own_feat.at[c, pl.ds(q * share, share)], src.at[c, far_first + q],
            afs.at[c, q], a1r.at[c], (far_first + q, other),
        )

    def scatter(c, q):
        return remote(
            own_feat.at[c, pl.ds(q * share, share)], src.at[c, first + q],
            a1s.at[c, q], a1r.at[c], (first + q, rep),
        )

    for c in range(slices):
        for q in range(nrep):
            @pl.when(sends_far(q))
            def _():
                scatter_far(c, q).start()

            @pl.when(sends_near(q))
            def _():
                scatter(c, q).start()

            @pl.when(jnp.logical_and(own_chunk, first + q == row))
            def _():
                local = pltpu.make_async_copy(
                    own_feat.at[c, pl.ds(q * share, share)], src.at[c, row], loc_sem
                )
                local.start()
                local.wait()

    def gather(c, d):
        to = ((hi + d) % half) * PAIR + lo
        return remote(
            src.at[c, row], src.at[c, row], a2s.at[c, d - 1], a2r.at[c, d - 1], (to, rep)
        )

    def share_pair(c, d):
        chunk = ((hi + half - d) % half) * PAIR + lo
        return remote(src.at[c, chunk], src.at[c, chunk], a3s.at[c, d], a3r.at[c, d], partner)

    for c in range(slices):
        @pl.when(jnp.logical_not(own_chunk))
        def _():
            remote(src.at[c, row], src.at[c, row], a1s.at[c, 0], a1r.at[c], partner).wait_recv()

        for d in range(1, half):
            gather(c, d).start()
        share_pair(c, 0).start()

    my_feat = feat[pl.ds(pl.multiple_of(rep * share, share), share), :]
    base[...] = jnp.dot(my_feat, wself[...], preferred_element_type=F32)
    run = deg.shape[1]
    for b in range(rows // run):
        line = jnp.broadcast_to(deg[b : b + 1, :].astype(F32), (run, run))
        deg_col[pl.ds(b * run, run), :] = line.T
    adj_copy.wait()

    def partial(c, q):
        total = jnp.zeros((share, lanes), F32)
        for j in range(here):
            a = adj[j, pl.ds(pl.multiple_of(q * share, share), share), :]
            f = src[c, pl.ds(j * nrep, nrep)].reshape(rows, lanes)
            total = total + jnp.dot(a, f, preferred_element_type=F32)
        return total

    def send_part(c, d):
        to = (rep + d) % nrep
        return remote(
            part.at[c, d - 1], part_in.at[c, d - 1], bs.at[c, d - 1], br.at[c, d - 1], (row, to)
        )

    for c in range(slices):
        for d in range(1, half):
            gather(c, d).wait_recv()
            share_pair(c, d).start()
        for d in range(half):
            share_pair(c, d).wait_recv()
        for d in range(1, nrep):
            part[c, d - 1] = partial(c, (rep + d) % nrep).astype(BF16)
            send_part(c, d).start()
    degree = deg_col[pl.ds(pl.multiple_of(rep * share, share), share), :]
    aggs = []
    for c in range(slices):
        total = partial(c, rep)
        for d in range(1, nrep):
            send_part(c, d).wait_recv()
            total = total + part_in[c, d - 1].astype(F32)
        aggs.append((total / degree).astype(BF16))
    agg = jnp.concatenate(aggs, axis=1)

    pre = base[...] + jnp.dot(agg, wneigh[...], preferred_element_type=F32)
    sig = jax.nn.sigmoid(pre)
    gpre = (cot[...].astype(F32) * sig * (1.0 + pre * (1.0 - sig))).astype(BF16)

    direct = [(step, way) for step in (1, 2) if step < nrep for way in (1, -1)]

    def within(k):
        return jnp.logical_and(k >= 0, k < nrep)

    def send_dagg(c, i):
        step, way = direct[i]
        return remote(
            dagg.at[c, rep], dagg.at[c, rep], cs.at[c, i], cr.at[c, rep], (row, rep + way * step)
        )

    def pass_dagg(c, d, way):
        origin = rep - way * d
        return remote(
            dagg.at[c, origin], dagg.at[c, origin], fs.at[c, origin], cr.at[c, origin], (row, rep + way)
        )

    def passes(d, way):
        return jnp.logical_and(within(rep - way * d), within(rep + way))

    for c in range(slices):
        back_t = lax.dot_general(
            gpre, wneigh[c * lanes : (c + 1) * lanes, :], (((1,), (1,)), ((), ())),
            preferred_element_type=F32,
        )
        dagg[c, rep] = (back_t / degree).astype(BF16)
        for i in reversed(range(len(direct))):
            @pl.when(within(rep + direct[i][1] * direct[i][0]))
            def _():
                send_dagg(c, i).start()
    ws = lax.dot_general(my_feat, gpre, (((0,), (0,)), ((), ())), preferred_element_type=F32)
    wn = lax.dot_general(agg, gpre, (((0,), (0,)), ((), ())), preferred_element_type=F32)
    piece = wpart.shape[1]
    wpart[pl.ds(0, half)] = ws.astype(BF16).reshape(half, piece, width)
    wpart[pl.ds(half, half)] = wn.astype(BF16).reshape(half, piece, width)

    def send_w1(d):
        to = (row + d) % nrow
        return remote(wpart.at[to], wrow_in.at[d - 1], w1s.at[d - 1], w1r.at[d - 1], (to, rep))

    for d in range(1, nrow):
        send_w1(d).start()
    out[...] = (pre * sig).astype(BF16)
    base[...] = lax.dot_general(gpre, wself[...], (((1,), (1,)), ((), ())), preferred_element_type=F32)

    unit = max(share, 128)
    per_unit = unit // share

    def send_pair(c, h):
        return remote(
            terms.at[c, h * PAIR + (1 - lo)], pair_in.at[c, h], d0s.at[c, h], d0r.at[c, h], partner
        )

    def send_plane(c, d):
        h = (hi + d) % half
        return remote(
            summed.at[c, h], plane_in.at[c, d - 1], d1s.at[c, d - 1], d1r.at[c, d - 1],
            (h * PAIR + lo, rep),
        )

    def to_owner(c):
        return remote(back.at[c], back_in.at[c], d2s.at[c], d2r.at[c], owner)

    def take_dagg(c, d):
        for way in (1, -1):
            @pl.when(within(rep - way * d))
            def _():
                origin = rep - way * d
                remote(
                    dagg.at[c, rep], dagg.at[c, origin], cs.at[c, 0], cr.at[c, origin], (row, rep)
                ).wait_recv()

            if d >= 2:
                @pl.when(passes(d, way))
                def _():
                    pass_dagg(c, d, way).start()

    def make_terms(c):
        dagg_t[...] = dagg[c].reshape(rows, lanes).T
        for u in range(here * rows // unit):
            j, col = divmod(u * unit, rows)
            t = jnp.dot(dagg_t[...], adj[j, :, col : col + unit], preferred_element_type=F32)
            terms[c, pl.ds(u * per_unit, per_unit)] = t.T.astype(BF16).reshape(per_unit, share, lanes)
            for r in range(u * per_unit, (u + 1) * per_unit):
                @pl.when(r % PAIR != lo)
                def _():
                    send_pair(c, r // PAIR).start()

    def add_pair(c):
        for d in list(range(1, half)) + [0]:
            h = (hi + d) % half
            send_pair(c, h).wait_recv()
            both = terms[c, h * PAIR + lo].astype(F32) + pair_in[c, h].astype(F32)
            if d > 0:
                summed[c, h] = both.astype(BF16)
                send_plane(c, d).start()
            else:
                back_sum[c] = both

    def add_plane(c):
        both = back_sum[c]
        for d in range(1, half):
            send_plane(c, d).wait_recv()
            both = both + plane_in[c, d - 1].astype(F32)
        back[c] = both.astype(BF16)

        @pl.when(moves)
        def _():
            to_owner(c).start()

    back_sum = {}
    for c in range(slices):
        for d in range(1, nrep):
            take_dagg(c, d)
        make_terms(c)
        if c + 1 < slices:
            add_pair(c)

    wsum = wpart[row].astype(F32)
    for d in range(1, nrow):
        send_w1(d).wait_recv()
        wsum = wsum + wrow_in[d - 1].astype(F32)
    wrep_in[rep] = wsum.astype(BF16)

    def send_w2(d):
        return remote(
            wrep_in.at[rep], wrep_in.at[rep], w2s.at[d - 1], w2r.at[d - 1], (row, (rep + d) % nrep)
        )

    for d in range(1, nrep):
        send_w2(d).start()
    add_pair(slices - 1)
    for c in range(slices - 1):
        add_plane(c)

    for d in range(1, nrep):
        remote(
            wrep_in.at[rep], wrep_in.at[(rep + nrep - d) % nrep], w2s.at[d - 1], w2r.at[d - 1], (row, rep)
        ).wait_recv()
    wsum = wrep_in[0].astype(F32)
    for k in range(1, nrep):
        wsum = wsum + wrep_in[k].astype(F32)
    wall[row] = wsum.astype(BF16)

    def send_w3(d):
        return remote(
            wall.at[row], wall.at[row], w3s.at[d - 1], w3r.at[d - 1], ((row + d) % nrow, rep)
        )

    for d in range(1, nrow):
        send_w3(d).start()
    add_plane(slices - 1)
    for d in range(1, nrow):
        remote(
            wall.at[row], wall.at[(row + nrow - d) % nrow], w3s.at[d - 1], w3r.at[d - 1], (row, rep)
        ).wait_recv()

    for c in range(slices):
        cols = slice(c * lanes, (c + 1) * lanes)

        @pl.when(moves)
        def _():
            to_owner(c).wait_recv()
            gfeat[:, cols] = (base[:, cols] + back_in[c].astype(F32)).astype(BF16)

        @pl.when(jnp.logical_not(moves))
        def _():
            gfeat[:, cols] = (base[:, cols] + back[c].astype(F32)).astype(BF16)

    for c in range(slices):
        for q in range(nrep):
            @pl.when(sends_near(q))
            def _():
                scatter(c, q).wait_send()

            @pl.when(sends_far(q))
            def _():
                scatter_far(c, q).wait_send()

        for d in range(1, half):
            gather(c, d).wait_send()
            send_plane(c, d).wait_send()
        for d in range(half):
            share_pair(c, d).wait_send()
            send_pair(c, d).wait_send()
        for d in range(1, nrep):
            send_part(c, d).wait_send()
        for i in range(len(direct)):
            @pl.when(within(rep + direct[i][1] * direct[i][0]))
            def _():
                send_dagg(c, i).wait_send()

        for d in range(2, nrep):
            for way in (1, -1):
                @pl.when(passes(d, way))
                def _():
                    pass_dagg(c, d, way).wait_send()

        @pl.when(moves)
        def _():
            to_owner(c).wait_send()

    for d in range(1, nrep):
        send_w2(d).wait_send()
    for d in range(1, nrow):
        send_w1(d).wait_send()
        send_w3(d).wait_send()


def close_kernel(out_in, wall, gfeat_in, out, gself, gneigh, gfeat):
    half = wall.shape[0] // 2
    out[...] = out_in[...]
    gfeat[...] = gfeat_in[...]
    gself[...] = wall[pl.ds(0, half)].reshape(gself.shape).astype(F32)
    gneigh[...] = wall[pl.ds(half, half)].reshape(gneigh.shape).astype(F32)


def body(
    nrow, nrep,
    features, weight_self, weight_neigh, degrees, tile_values, tile_blocks, tile_count, cotangent,
):
    rows, width = features.shape
    here = tile_values.shape[1]
    tile = tile_values.shape[-1]
    share = rows // nrep
    half = nrow // PAIR
    piece = 2 * width // nrow
    lanes = 128
    slices = width // lanes
    adjacency = dense_adjacency(
        tile_values[0], tile_blocks.transpose(0, 1, 3, 2)[0], tile_count[0], rows
    )
    sems = pltpu.SemaphoreType.DMA
    vmem = pl.BlockSpec(memory_space=pltpu.VMEM)

    def buf(*shape):
        return pltpu.VMEM(shape, BF16)

    out, wall, gfeat = pl.pallas_call(
        functools.partial(layer_kernel, nrow, nrep, here),
        out_shape=(
            jax.ShapeDtypeStruct((share, width), BF16),
            jax.ShapeDtypeStruct((nrow, piece, width), BF16),
            jax.ShapeDtypeStruct((share, width), BF16),
        ),
        in_specs=[vmem] * 5 + [pl.BlockSpec(memory_space=pl.ANY)],
        out_specs=(vmem,) * 3,
        scratch_shapes=[
            buf(here, rows, rows),
            buf(slices, rows, lanes),
            buf(slices, nrow, share, lanes),
            buf(slices, nrep - 1, share, lanes),
            buf(slices, nrep - 1, share, lanes),
            buf(slices, nrep, share, lanes),
            buf(lanes, rows),
            buf(slices, nrow, share, lanes),
            buf(slices, half, share, lanes),
            buf(slices, half, share, lanes),
            buf(slices, half - 1, share, lanes),
            buf(slices, share, lanes),
            buf(slices, share, lanes),
            buf(nrow, piece, width),
            buf(nrow - 1, piece, width),
            buf(nrep, piece, width),
            pltpu.VMEM((share, width), F32),
            pltpu.VMEM((rows, tile), F32),
            sems, sems,
            sems((slices, nrep)), sems((slices, nrep)), sems((slices,)),
            sems((slices, half - 1)), sems((slices, half - 1)),
            sems((slices, half)), sems((slices, half)),
            sems((slices, nrep - 1)), sems((slices, nrep - 1)),
            sems((slices, 4)), sems((slices, nrep)), sems((slices, nrep)),
            sems((nrow - 1,)), sems((nrow - 1,)),
            sems((nrep - 1,)), sems((nrep - 1,)),
            sems((nrow - 1,)), sems((nrow - 1,)),
            sems((slices, half)), sems((slices, half)),
            sems((slices, half - 1)), sems((slices, half - 1)),
            sems((slices,)), sems((slices,)),
        ],
        compiler_params=pltpu.CompilerParams(collective_id=0, has_side_effects=True),
        name="layer",
    )(features, weight_self, weight_neigh, degrees.reshape(rows // tile, tile), cotangent, adjacency)
    out, grad_self, grad_neigh, gfeat = pl.pallas_call(
        close_kernel,
        out_shape=(
            jax.ShapeDtypeStruct((share, width), BF16),
            jax.ShapeDtypeStruct((width, width), F32),
            jax.ShapeDtypeStruct((width, width), F32),
            jax.ShapeDtypeStruct((share, width), BF16),
        ),
        in_specs=[vmem] * 3,
        out_specs=(vmem,) * 4,
        name="close",
    )(out, wall, gfeat)
    return out, grad_self, grad_neigh, gfeat


def solution(mesh):
    in_specs = (
        P("row", None),
        P(),
        P(),
        P("row"),
        P("row", "rep", None, None, None),
        P("row", "rep", None, None),
        P("row", "rep"),
        P(("row", "rep"), None),
    )
    out_specs = (P(("row", "rep"), None), P(), P(), P(("row", "rep"), None))
    run = functools.partial(body, mesh.shape["row"], mesh.shape["rep"])
    return jax.shard_map(run, mesh=mesh, in_specs=in_specs, out_specs=out_specs, check_vma=False)
```

```python
import functools

import jax
import jax.numpy as jnp
from jax import lax
from jax.experimental import pallas as pl
from jax.experimental.pallas import tpu as pltpu
from jax.sharding import PartitionSpec as P

MESH = pl.DeviceIdType.MESH
F32 = jnp.float32
BF16 = jnp.bfloat16
PAIR = 2


def dense_kernel(blocks_ref, count_ref, tiles_ref, out_ref, acc):
    section = pl.program_id(0)
    tile = tiles_ref.shape[-1]
    acc[...] = jnp.zeros_like(acc)

    def add(slot, carry):
        to = pl.multiple_of(blocks_ref[section, 0, slot] * tile, tile)
        src = pl.multiple_of(blocks_ref[section, 1, slot] * tile, tile)
        acc[pl.ds(to, tile), pl.ds(src, tile)] += tiles_ref[0, slot].astype(F32)
        return carry

    lax.fori_loop(0, count_ref[section], add, 0)
    out_ref[0] = acc[...].astype(BF16)


def dense_adjacency(tile_values, tile_blocks, tile_count, rows):
    sections, slots, tile, _ = tile_values.shape
    return pl.pallas_call(
        dense_kernel,
        grid=(sections,),
        out_shape=jax.ShapeDtypeStruct((sections, rows, rows), BF16),
        in_specs=[
            pl.BlockSpec(memory_space=pltpu.SMEM),
            pl.BlockSpec(memory_space=pltpu.SMEM),
            pl.BlockSpec((1, slots, tile, tile), lambda s: (s, 0, 0, 0)),
        ],
        out_specs=pl.BlockSpec((1, rows, rows), lambda s: (s, 0, 0)),
        scratch_shapes=[pltpu.VMEM((rows, rows), F32)],
        name="dense",
    )(tile_blocks, tile_count, tile_values)


def remote(src, dst, send, recv, device):
    return pltpu.make_async_remote_copy(
        src_ref=src, dst_ref=dst, send_sem=send, recv_sem=recv, device_id=device, device_id_type=MESH
    )


def layer_kernel(
    nrow, nrep, here,
    feat, wself, wneigh, deg, cot, adj_hbm,
    out, wall, gfeat,
    adj, own_feat, src, part, part_in, dagg, dagg_t, terms, pair_in, summed, plane_in, back, back_in,
    wpart, wrow_in, wrep_in, base, deg_col,
    adj_sem, loc_sem, afs, a1s, a1r, a2s, a2r, a3s, a3r, bs, br, cs, cr, w1s, w1r, w2s, w2r, w3s, w3r,
    d0s, d0r, d1s, d1r, d2s, d2r,
):
    row, rep = lax.axis_index("row"), lax.axis_index("rep")
    rows, width = feat.shape
    lanes = src.shape[-1]
    slices = width // lanes
    share = rows // nrep
    half = nrow // PAIR
    hi, lo = row // PAIR, row % PAIR
    partner = (hi * PAIR + (1 - lo), rep)
    owner = (rep * here + row // nrep, row % nrep)
    giver = ((row % here) * nrep + rep, row // here)
    moves = jnp.logical_or(owner[0] != row, owner[1] != rep)

    adj_copy = pltpu.make_async_copy(adj_hbm, adj, adj_sem)
    adj_copy.start()

    barrier = pltpu.get_barrier_semaphore()

    def greet(device):
        pl.semaphore_signal(barrier, inc=1, device_id=device, device_id_type=MESH)

    for d in range(1, nrow):
        greet(((row + d) % nrow, rep))
    for d in range(1, nrep):
        greet((row, (rep + d) % nrep))

    @pl.when(moves)
    def _():
        greet(owner)
        greet(giver)

    def is_far(r, k):
        return r // PAIR == half - 1 - (k * here) // PAIR

    other = (rep + nrep - nrep // 2) % nrep
    far_first = (row - other * here) * nrep
    serves_far = row // here == other
    far_me = is_far(row, rep)
    far_source = (rep * here + row // nrep, (rep + nrep // 2) % nrep)

    def sends_far(q):
        return jnp.logical_and(serves_far, is_far(far_first + q, other))

    expected = nrow - 1 + nrep - 1 + 2 * moves.astype(jnp.int32) + far_me.astype(jnp.int32)
    for q in range(nrep):
        expected = expected + sends_far(q).astype(jnp.int32)

        @pl.when(sends_far(q))
        def _():
            greet((far_first + q, other))

    @pl.when(far_me)
    def _():
        greet(far_source)

    for c in range(slices):
        own_feat[c] = feat[:, c * lanes : (c + 1) * lanes]

    pl.semaphore_wait(barrier, expected)

    is_source = row // here == rep
    first = (row - rep * here) * nrep
    own_chunk = jnp.logical_and(row == rep * here + row // nrep, jnp.logical_not(far_me))

    def sends_near(q):
        near = jnp.logical_and(is_source, jnp.logical_not(is_far(first + q, rep)))
        return jnp.logical_and(near, first + q != row)

    def scatter_far(c, q):
        return remote(
            own_feat.at[c, pl.ds(q * share, share)], src.at[c, far_first + q],
            afs.at[c, q], a1r.at[c], (far_first + q, other),
        )

    def scatter(c, q):
        return remote(
            own_feat.at[c, pl.ds(q * share, share)], src.at[c, first + q],
            a1s.at[c, q], a1r.at[c], (first + q, rep),
        )

    for c in range(slices):
        for q in range(nrep):
            @pl.when(sends_far(q))
            def _():
                scatter_far(c, q).start()

            @pl.when(sends_near(q))
            def _():
                scatter(c, q).start()

            @pl.when(jnp.logical_and(own_chunk, first + q == row))
            def _():
                local = pltpu.make_async_copy(
                    own_feat.at[c, pl.ds(q * share, share)], src.at[c, row], loc_sem
                )
                local.start()
                local.wait()

    def gather(c, d):
        to = ((hi + d) % half) * PAIR + lo
        return remote(
            src.at[c, row], src.at[c, row], a2s.at[c, d - 1], a2r.at[c, d - 1], (to, rep)
        )

    def share_pair(c, d):
        chunk = ((hi + half - d) % half) * PAIR + lo
        return remote(src.at[c, chunk], src.at[c, chunk], a3s.at[c, d], a3r.at[c, d], partner)

    for c in range(slices):
        @pl.when(jnp.logical_not(own_chunk))
        def _():
            remote(src.at[c, row], src.at[c, row], a1s.at[c, 0], a1r.at[c], partner).wait_recv()

        for d in range(1, half):
            gather(c, d).start()
        share_pair(c, 0).start()

    my_feat = feat[pl.ds(pl.multiple_of(rep * share, share), share), :]
    base[...] = jnp.dot(my_feat, wself[...], preferred_element_type=F32)
    run = deg.shape[1]
    for b in range(rows // run):
        line = jnp.broadcast_to(deg[b : b + 1, :].astype(F32), (run, run))
        deg_col[pl.ds(b * run, run), :] = line.T
    adj_copy.wait()

    def partial(c, q):
        total = jnp.zeros((share, lanes), F32)
        for j in range(here):
            a = adj[j, pl.ds(pl.multiple_of(q * share, share), share), :]
            f = src[c, pl.ds(j * nrep, nrep)].reshape(rows, lanes)
            total = total + jnp.dot(a, f, preferred_element_type=F32)
        return total

    def send_part(c, d):
        to = (rep + d) % nrep
        return remote(
            part.at[c, d - 1], part_in.at[c, d - 1], bs.at[c, d - 1], br.at[c, d - 1], (row, to)
        )

    for c in range(slices):
        for d in range(1, half):
            gather(c, d).wait_recv()
            share_pair(c, d).start()
        for d in range(half):
            share_pair(c, d).wait_recv()
        for d in range(1, nrep):
            part[c, d - 1] = partial(c, (rep + d) % nrep).astype(BF16)
            send_part(c, d).start()
    degree = deg_col[pl.ds(pl.multiple_of(rep * share, share), share), :]
    aggs = []
    for c in range(slices):
        total = partial(c, rep)
        for d in range(1, nrep):
            send_part(c, d).wait_recv()
            total = total + part_in[c, d - 1].astype(F32)
        aggs.append((total / degree).astype(BF16))
    agg = jnp.concatenate(aggs, axis=1)

    pre = base[...] + jnp.dot(agg, wneigh[...], preferred_element_type=F32)
    sig = jax.nn.sigmoid(pre)
    gpre = (cot[...].astype(F32) * sig * (1.0 + pre * (1.0 - sig))).astype(BF16)

    def send_dagg(c, d):
        return remote(
            dagg.at[c, rep], dagg.at[c, rep], cs.at[c, d - 1], cr.at[c, d - 1],
            (row, (rep + d) % nrep),
        )

    for c in range(slices):
        back_t = lax.dot_general(
            gpre, wneigh[c * lanes : (c + 1) * lanes, :], (((1,), (1,)), ((), ())),
            preferred_element_type=F32,
        )
        dagg[c, rep] = (back_t / degree).astype(BF16)
        for d in range(1, nrep):
            send_dagg(c, d).start()
    ws = lax.dot_general(my_feat, gpre, (((0,), (0,)), ((), ())), preferred_element_type=F32)
    wn = lax.dot_general(agg, gpre, (((0,), (0,)), ((), ())), preferred_element_type=F32)
    piece = wpart.shape[1]
    wpart[pl.ds(0, half)] = ws.astype(BF16).reshape(half, piece, width)
    wpart[pl.ds(half, half)] = wn.astype(BF16).reshape(half, piece, width)

    def send_w1(d):
        to = (row + d) % nrow
        return remote(wpart.at[to], wrow_in.at[d - 1], w1s.at[d - 1], w1r.at[d - 1], (to, rep))

    for d in range(1, nrow):
        send_w1(d).start()
    out[...] = (pre * sig).astype(BF16)
    base[...] = lax.dot_general(gpre, wself[...], (((1,), (1,)), ((), ())), preferred_element_type=F32)

    unit = max(share, 128)
    per_unit = unit // share

    def send_pair(c, h):
        return remote(
            terms.at[c, h * PAIR + (1 - lo)], pair_in.at[c, h], d0s.at[c, h], d0r.at[c, h], partner
        )

    def send_plane(c, d):
        h = (hi + d) % half
        return remote(
            summed.at[c, h], plane_in.at[c, d - 1], d1s.at[c, d - 1], d1r.at[c, d - 1],
            (h * PAIR + lo, rep),
        )

    def to_owner(c):
        return remote(back.at[c], back_in.at[c], d2s.at[c], d2r.at[c], owner)

    def make_terms(c):
        for d in range(1, nrep):
            remote(
                dagg.at[c, rep], dagg.at[c, (rep + nrep - d) % nrep], cs.at[c, d - 1], cr.at[c, d - 1],
                (row, rep),
            ).wait_recv()
        dagg_t[...] = dagg[c].reshape(rows, lanes).T
        for u in range(here * rows // unit):
            j, col = divmod(u * unit, rows)
            t = jnp.dot(dagg_t[...], adj[j, :, col : col + unit], preferred_element_type=F32)
            terms[c, pl.ds(u * per_unit, per_unit)] = t.T.astype(BF16).reshape(per_unit, share, lanes)
            for r in range(u * per_unit, (u + 1) * per_unit):
                @pl.when(r % PAIR != lo)
                def _():
                    send_pair(c, r // PAIR).start()

    def add_pair(c):
        for d in list(range(1, half)) + [0]:
            h = (hi + d) % half
            send_pair(c, h).wait_recv()
            both = terms[c, h * PAIR + lo].astype(F32) + pair_in[c, h].astype(F32)
            if d > 0:
                summed[c, h] = both.astype(BF16)
                send_plane(c, d).start()
            else:
                back_sum[c] = both

    def add_plane(c):
        both = back_sum[c]
        for d in range(1, half):
            send_plane(c, d).wait_recv()
            both = both + plane_in[c, d - 1].astype(F32)
        back[c] = both.astype(BF16)

        @pl.when(moves)
        def _():
            to_owner(c).start()

    back_sum = {}
    for c in range(slices):
        make_terms(c)
        if c + 1 < slices:
            add_pair(c)

    wsum = wpart[row].astype(F32)
    for d in range(1, nrow):
        send_w1(d).wait_recv()
        wsum = wsum + wrow_in[d - 1].astype(F32)
    wrep_in[rep] = wsum.astype(BF16)

    def send_w2(d):
        return remote(
            wrep_in.at[rep], wrep_in.at[rep], w2s.at[d - 1], w2r.at[d - 1], (row, (rep + d) % nrep)
        )

    for d in range(1, nrep):
        send_w2(d).start()
    add_pair(slices - 1)
    for c in range(slices - 1):
        add_plane(c)

    for d in range(1, nrep):
        remote(
            wrep_in.at[rep], wrep_in.at[(rep + nrep - d) % nrep], w2s.at[d - 1], w2r.at[d - 1], (row, rep)
        ).wait_recv()
    wsum = wrep_in[0].astype(F32)
    for k in range(1, nrep):
        wsum = wsum + wrep_in[k].astype(F32)
    wall[row] = wsum.astype(BF16)

    def send_w3(d):
        return remote(
            wall.at[row], wall.at[row], w3s.at[d - 1], w3r.at[d - 1], ((row + d) % nrow, rep)
        )

    for d in range(1, nrow):
        send_w3(d).start()
    add_plane(slices - 1)
    for d in range(1, nrow):
        remote(
            wall.at[row], wall.at[(row + nrow - d) % nrow], w3s.at[d - 1], w3r.at[d - 1], (row, rep)
        ).wait_recv()

    for c in range(slices):
        cols = slice(c * lanes, (c + 1) * lanes)

        @pl.when(moves)
        def _():
            to_owner(c).wait_recv()
            gfeat[:, cols] = (base[:, cols] + back_in[c].astype(F32)).astype(BF16)

        @pl.when(jnp.logical_not(moves))
        def _():
            gfeat[:, cols] = (base[:, cols] + back[c].astype(F32)).astype(BF16)

    for c in range(slices):
        for q in range(nrep):
            @pl.when(sends_near(q))
            def _():
                scatter(c, q).wait_send()

            @pl.when(sends_far(q))
            def _():
                scatter_far(c, q).wait_send()

        for d in range(1, half):
            gather(c, d).wait_send()
            send_plane(c, d).wait_send()
        for d in range(half):
            share_pair(c, d).wait_send()
            send_pair(c, d).wait_send()
        for d in range(1, nrep):
            send_part(c, d).wait_send()
            send_dagg(c, d).wait_send()

        @pl.when(moves)
        def _():
            to_owner(c).wait_send()

    for d in range(1, nrep):
        send_w2(d).wait_send()
    for d in range(1, nrow):
        send_w1(d).wait_send()
        send_w3(d).wait_send()


def close_kernel(out_in, wall, gfeat_in, out, gself, gneigh, gfeat):
    half = wall.shape[0] // 2
    out[...] = out_in[...]
    gfeat[...] = gfeat_in[...]
    gself[...] = wall[pl.ds(0, half)].reshape(gself.shape).astype(F32)
    gneigh[...] = wall[pl.ds(half, half)].reshape(gneigh.shape).astype(F32)


def body(
    nrow, nrep,
    features, weight_self, weight_neigh, degrees, tile_values, tile_blocks, tile_count, cotangent,
):
    rows, width = features.shape
    here = tile_values.shape[1]
    tile = tile_values.shape[-1]
    share = rows // nrep
    half = nrow // PAIR
    piece = 2 * width // nrow
    lanes = 128
    slices = width // lanes
    adjacency = dense_adjacency(
        tile_values[0], tile_blocks.transpose(0, 1, 3, 2)[0], tile_count[0], rows
    )
    sems = pltpu.SemaphoreType.DMA
    vmem = pl.BlockSpec(memory_space=pltpu.VMEM)

    def buf(*shape):
        return pltpu.VMEM(shape, BF16)

    out, wall, gfeat = pl.pallas_call(
        functools.partial(layer_kernel, nrow, nrep, here),
        out_shape=(
            jax.ShapeDtypeStruct((share, width), BF16),
            jax.ShapeDtypeStruct((nrow, piece, width), BF16),
            jax.ShapeDtypeStruct((share, width), BF16),
        ),
        in_specs=[vmem] * 5 + [pl.BlockSpec(memory_space=pl.ANY)],
        out_specs=(vmem,) * 3,
        scratch_shapes=[
            buf(here, rows, rows),
            buf(slices, rows, lanes),
            buf(slices, nrow, share, lanes),
            buf(slices, nrep - 1, share, lanes),
            buf(slices, nrep - 1, share, lanes),
            buf(slices, nrep, share, lanes),
            buf(lanes, rows),
            buf(slices, nrow, share, lanes),
            buf(slices, half, share, lanes),
            buf(slices, half, share, lanes),
            buf(slices, half - 1, share, lanes),
            buf(slices, share, lanes),
            buf(slices, share, lanes),
            buf(nrow, piece, width),
            buf(nrow - 1, piece, width),
            buf(nrep, piece, width),
            pltpu.VMEM((share, width), F32),
            pltpu.VMEM((rows, tile), F32),
            sems, sems,
            sems((slices, nrep)), sems((slices, nrep)), sems((slices,)),
            sems((slices, half - 1)), sems((slices, half - 1)),
            sems((slices, half)), sems((slices, half)),
            sems((slices, nrep - 1)), sems((slices, nrep - 1)),
            sems((slices, nrep - 1)), sems((slices, nrep - 1)),
            sems((nrow - 1,)), sems((nrow - 1,)),
            sems((nrep - 1,)), sems((nrep - 1,)),
            sems((nrow - 1,)), sems((nrow - 1,)),
            sems((slices, half)), sems((slices, half)),
            sems((slices, half - 1)), sems((slices, half - 1)),
            sems((slices,)), sems((slices,)),
        ],
        compiler_params=pltpu.CompilerParams(collective_id=0, has_side_effects=True),
        name="layer",
    )(features, weight_self, weight_neigh, degrees.reshape(rows // tile, tile), cotangent, adjacency)
    out, grad_self, grad_neigh, gfeat = pl.pallas_call(
        close_kernel,
        out_shape=(
            jax.ShapeDtypeStruct((share, width), BF16),
            jax.ShapeDtypeStruct((width, width), F32),
            jax.ShapeDtypeStruct((width, width), F32),
            jax.ShapeDtypeStruct((share, width), BF16),
        ),
        in_specs=[vmem] * 3,
        out_specs=(vmem,) * 4,
        name="close",
    )(out, wall, gfeat)
    return out, grad_self, grad_neigh, gfeat


def solution(mesh):
    in_specs = (
        P("row", None),
        P(),
        P(),
        P("row"),
        P("row", "rep", None, None, None),
        P("row", "rep", None, None),
        P("row", "rep"),
        P(("row", "rep"), None),
    )
    out_specs = (P(("row", "rep"), None), P(), P(), P(("row", "rep"), None))
    run = functools.partial(body, mesh.shape["row"], mesh.shape["rep"])
    return jax.shard_map(run, mesh=mesh, in_specs=in_specs, out_specs=out_specs, check_vma=False)
```
